32 devices in a mesh: groups: 2 (over y), ctx: 8 (over z, x), head: 2 (over core).
Axes of the slice: x: 2, y: 2, z: 4, core: 2. Of those that a mesh axis runs over, the one named last changes fastest.
Arguments:
- keys_values: bfloat16 [2, 8192, 1024], P(None, ('groups', 'ctx'), 'head'), parts along dimension 1, may hold values from -6 to 6
- span_order: int32 [32], P('groups'), parts along dimension 0, may hold values from 0 to 15, as said below
- page_table: int32 [64], P('groups'), parts along dimension 0, may hold values from 0 to 31, as said below
Outputs:
- paged_cache: bfloat16 [2, 64, 128, 1024], P(None, ('groups', 'ctx', 'head')), parts along dimension 1
The draws below stay inside these ranges and needn't reach their ends.
There are 2 independent parts, one for each index of `groups`. The reference program is written for one: setup_inputs(seed, part) draws one part's arguments, and reference() takes and returns one part's arrays. A program takes and returns all parts, laid end to end along the dimension named above; each array names one. Nothing has to cross between parts.
Inputs may be any that keep to these rules, and one draw needn't show every extreme that they name: `span_order`: blocks 2 c and 2 c + 1 hold two spans whose numbers add to 15; every span is held once. A permutation of the slots in which page p goes to a slot of p // 2, that is page_table[p] // 2 == p // 2.
All inputs are finite; a program needn't handle non-finite values.
Results may differ from the reference program's by a relative error of at most 0.001.
Values may be sent and summed in bfloat16 or wider, within the bound.
No kernel may reach another device: no remote copies, remote signals or barrier semaphores. Data moves between devices by JAX's collectives and lax.ppermute only.
A program may use at most 64 MiB of HBM per device.

```python
import jax
import jax.numpy as jnp

KVH = 8
HD = 128
PAGE = 128
SPAN = 256
SPANS = 16
TOKENS = 4096
PAGES = 32
PAGES_SHARD = 2


def draw_span_order(key, part):
    halves = SPANS // 2
    lower = jax.random.permutation(jax.random.fold_in(key, 11), halves).astype(jnp.int32)
    flipped = jax.random.randint(jax.random.fold_in(key, 12), (halves,), 0, 2)
    first = jnp.where(flipped == 1, SPANS - 1 - lower, lower)
    second = SPANS - 1 - first
    return jnp.stack([first, second], axis=1).reshape(SPANS).astype(jnp.int32)


def draw_page_table(key, part):
    shards = PAGES // PAGES_SHARD
    ranks = jax.random.randint(jax.random.fold_in(key, 21), (shards, PAGES_SHARD), 0, 1048576)
    ranks = ranks * PAGES_SHARD + jnp.arange(PAGES_SHARD, dtype=jnp.int32)[None, :]
    local_slots = jnp.argsort(ranks, axis=1).astype(jnp.int32)
    table = local_slots + jnp.arange(shards, dtype=jnp.int32)[:, None] * PAGES_SHARD
    return table.reshape(PAGES).astype(jnp.int32)


def block_levels(key, extent, pieces, least, high):
    gain = 1.0
    for dim, blocks in pieces:
        draws = jax.random.uniform(jax.random.fold_in(jax.random.fold_in(key, 6), dim), (blocks,), jnp.float32, least / len(pieces), high / len(pieces))
        gain = gain * jnp.repeat(jnp.exp(draws), extent[dim] // blocks).reshape((-1,) + (1,) * (len(extent) - 1 - dim))
    return gain


def gaussian(stream_key, dims, scale, reach, split=(), kind=jnp.bfloat16):
    level = block_levels(stream_key, dims, split, -0.22, 0.18) if split else 1.0
    drawn = jax.random.normal(stream_key, dims, jnp.float32) * scale * level
    return jnp.minimum(jnp.maximum(drawn, -reach), reach).astype(kind)


def setup_inputs(seed: int = 0, part: int = 0) -> dict:
    key_list = jax.random.split(jax.random.key(seed), 4)
    part_keys = jax.random.split(jax.random.fold_in(key_list[3], part), 4)
    return {
        "keys_values": gaussian(part_keys[0], (2, TOKENS, KVH * HD), 1.0, 6.0, ((1, 8), (2, 2))),
        "span_order": draw_span_order(jax.random.fold_in(jax.random.fold_in(key_list[3], part), 71), part),
        "page_table": draw_page_table(jax.random.fold_in(jax.random.fold_in(key_list[3], part), 71), part),
    }


def reference(keys_values, span_order, page_table):
    blocks = keys_values.reshape(2, SPANS, SPAN, KVH * HD)
    context = jnp.zeros_like(blocks).at[:, span_order].set(blocks)
    page_rows = context.reshape(2, PAGES, PAGE, KVH * HD)
    paged_cache = jnp.zeros_like(page_rows).at[:, page_table].set(page_rows)
    return paged_cache
```

```python
import jax
import jax.numpy as jnp
from jax import lax
from jax.sharding import PartitionSpec as P

PAGE = 128


def per_device(keys_values, span_order, page_table):
    tok_rows = keys_values.shape[1]
    width = keys_values.shape[2]
    span_len = tok_rows // 2
    per_span = span_len // PAGE
    ctx_index = lax.axis_index("ctx")
    spans = lax.axis_size("ctx") * lax.axis_size("head")
    half = spans // 2
    piece = span_len // half

    first_span = lax.dynamic_index_in_dim(span_order, 2 * ctx_index, keepdims=False)
    swap = first_span >= half
    blocks = keys_values.reshape(2, 2, half, piece, width)
    low = jnp.where(swap, blocks[:, 1], blocks[:, 0])
    high = jnp.where(swap, blocks[:, 0], blocks[:, 1])
    spread = jnp.stack([low, high], axis=0).transpose(0, 2, 1, 3, 4)
    spread = spread.reshape(spans, 2, piece, width)
    spread = lax.all_to_all(spread, ("ctx", "head"), split_axis=0, concat_axis=0, tiled=True)

    device = 2 * ctx_index + lax.axis_index("head")
    base = (device // half) * half
    wanted = base + jnp.arange(half, dtype=jnp.int32)
    chips = jnp.arange(spans, dtype=jnp.int32) // 2
    holder = jnp.sum(jnp.where(span_order[None, :] == wanted[:, None], chips[None, :], 0), axis=1)
    spread = spread.reshape(half, 2, 2, piece, width)
    routed = jnp.take(spread, holder, axis=0, mode="clip")
    groups = [list(range(half)), list(range(half, spans))]
    routed = lax.all_to_all(
        routed, ("ctx", "head"), split_axis=0, concat_axis=0, tiled=True, axis_index_groups=groups
    )
    rows = routed.transpose(2, 0, 3, 1, 4).reshape(2, per_span, PAGE, 2 * width)
    slots = lax.dynamic_slice_in_dim(page_table, device * per_span, per_span) - device * per_span
    order = jnp.sum(
        jnp.where(
            slots[None, :] == jnp.arange(per_span, dtype=jnp.int32)[:, None],
            jnp.arange(per_span, dtype=jnp.int32)[None, :],
            0,
        ),
        axis=1,
    )
    return jnp.take(rows, order, axis=1, mode="clip")


def solution(mesh):
    in_specs = (P(None, ("groups", "ctx"), "head"), P("groups"), P("groups"))
    out_specs = P(None, ("groups", "ctx", "head"), None, None)
    return jax.shard_map(
        per_device, mesh=mesh, in_specs=in_specs, out_specs=out_specs, check_vma=False
    )
```

```python
import functools

import jax
import jax.numpy as jnp
from jax import lax
from jax.experimental import pallas as pl
from jax.experimental.pallas import tpu as pltpu
from jax.sharding import PartitionSpec as P

PAGE = 128
SUBLANES = 16
AXES = ("ctx", "head")
VMEM = pl.BlockSpec(memory_space=pltpu.VMEM)
SMEM = pl.BlockSpec(memory_space=pltpu.SMEM)
SMALL = pltpu.CompilerParams(vmem_limit_bytes=8 << 20)
HBM = pl.BlockSpec(memory_space=pl.ANY)


def swap(x, distance, size):
    return lax.ppermute(x, AXES, [(i, i ^ distance) for i in range(size)])


def prepare(chips, piece, spans, data, *refs):
    outs, sems = refs[:-1], refs[-1]
    near = chips // 2
    me = lax.axis_index("ctx")
    mine_low = me < near
    first_low = spans[2 * me] < chips
    stay = jnp.where(mine_low == first_low, 0, 1)
    rows = near * piece
    copies = []

    def piece_at(block, target):
        start = block * rows + lax.rem(target, near) * piece
        return pl.ds(pl.multiple_of(start, piece), piece)

    n = 0
    for kind in range(2):
        for d in range(near, chips):
            src = data.at[kind, piece_at(1 - stay, me ^ d), :]
            copies.append(pltpu.make_async_copy(src, outs[n], sems.at[n]))
            n += 1
    for d in range(near):
        src = data.at[:, piece_at(stay, me ^ d), :]
        copies.append(pltpu.make_async_copy(src, outs[n], sems.at[n]))
        n += 1
    for copy in copies:
        copy.start()
    for copy in copies:
        copy.wait()


def route(chips, kind, spans, *refs):
    near = chips // 2
    ins, outs = refs[:chips], refs[chips:]
    me = lax.axis_index("ctx")
    local = lax.rem(me, near)
    low = me < near
    for d in range(chips):
        source = me ^ d
        a, b = spans[2 * source], spans[2 * source + 1]
        span = jnp.where((a < chips) == low, a, b)
        parity = lax.rem(span, 2)
        distance = lax.rem(span // 2, near) ^ local
        for j in range(near):

            @pl.when(distance == j)
            def _(d=d, j=j):
                outs[j][parity] = ins[d][kind] if d < near else ins[d][...]


def hand_over(near, *refs):
    ins, out = refs[:near], refs[near]
    other = 1 - lax.axis_index("head")
    for j in range(near):
        out[j] = ins[j][other]


def finish(near, piece, table, *refs):
    per_span = near * piece // PAGE
    own = [refs[:near], refs[near : 2 * near]]
    got = refs[2 * near : 2 * near + 2]
    out, sems = refs[2 * near + 2 :]
    me = lax.axis_index("ctx")
    head = lax.axis_index("head")
    width = out.shape[3] // 2
    device = 2 * me + head
    local = lax.rem(me, near)
    copies = []
    for kind in range(2):
        for j in range(near):
            row = (local ^ j) * piece
            slot = table[device * per_span + row // PAGE] - device * per_span
            rows = pl.ds(pl.multiple_of(lax.rem(row, PAGE), piece), piece)
            for k, (src, side) in enumerate(
                ((own[kind][j].at[head], head), (got[kind].at[j], 1 - head))
            ):
                cols = pl.ds(pl.multiple_of(side * width, width), width)
                dst = out.at[kind, slot, rows, cols]
                copies.append(pltpu.make_async_copy(src, dst, sems.at[len(copies)]))
    for copy in copies:
        copy.start()
    for copy in copies:
        copy.wait()


def by_permutes(keys_values, span_order, page_table):
    chips = lax.axis_size("ctx")
    size = 2 * chips
    near = chips // 2
    width = keys_values.shape[2]
    span_len = keys_values.shape[1] // 2
    piece = span_len // near
    dtype = keys_values.dtype
    one = jax.ShapeDtypeStruct((piece, width), dtype)
    two = jax.ShapeDtypeStruct((2, piece, width), dtype)
    n = 2 * near + near
    pieces = pl.pallas_call(
        functools.partial(prepare, chips, piece),
        out_shape=[one] * (2 * near) + [two] * near,
        in_specs=[SMEM, HBM],
        out_specs=[VMEM] * n,
        scratch_shapes=[pltpu.SemaphoreType.DMA((n,))],
        name="prepare",
            compiler_params=SMALL,
    )(span_order, keys_values)
    far = [
        [swap(pieces[kind * near + i], 2 * (near + i), size) for i in range(near)]
        for kind in range(2)
    ]
    stay = [pieces[2 * near]] + [swap(pieces[2 * near + d], 2 * d, size) for d in range(1, near)]
    own, got = [], []
    for kind in range(2):
        routed = pl.pallas_call(
            functools.partial(route, chips, kind),
            out_shape=[two] * near,
            in_specs=[SMEM] + [VMEM] * chips,
            out_specs=[VMEM] * near,
            name="route",
            compiler_params=SMALL,
        )(span_order, *stay, *far[kind])
        held = [routed[0]] + [swap(routed[j], 2 * j, size) for j in range(1, near)]
        send = pl.pallas_call(
            functools.partial(hand_over, near),
            out_shape=jax.ShapeDtypeStruct((near, piece, width), dtype),
            in_specs=[VMEM] * near,
            out_specs=VMEM,
            name="hand_over",
            compiler_params=SMALL,
        )(*held)
        own += held
        got.append(swap(send, 1, size))
    return pl.pallas_call(
        functools.partial(finish, near, piece),
        out_shape=jax.ShapeDtypeStruct((2, span_len // PAGE, PAGE, 2 * width), dtype),
        in_specs=[SMEM] + [VMEM] * (2 * near + 2),
        out_specs=HBM,
        scratch_shapes=[pltpu.SemaphoreType.DMA((4 * near,))],
        name="finish",
            compiler_params=SMALL,
    )(page_table, *own, *got)


def by_all_to_alls(keys_values, span_order, page_table):
    tok_rows = keys_values.shape[1]
    width = keys_values.shape[2]
    span_len = tok_rows // 2
    per_span = span_len // PAGE
    ctx_index = lax.axis_index("ctx")
    spans = lax.axis_size("ctx") * lax.axis_size("head")
    half = spans // 2
    piece = span_len // half

    first_span = lax.dynamic_index_in_dim(span_order, 2 * ctx_index, keepdims=False)
    flip = first_span >= half
    blocks = keys_values.reshape(2, 2, half, piece, width)
    low = jnp.where(flip, blocks[:, 1], blocks[:, 0])
    high = jnp.where(flip, blocks[:, 0], blocks[:, 1])
    spread = jnp.stack([low, high], axis=0).transpose(0, 2, 1, 3, 4)
    spread = spread.reshape(spans, 2, piece, width)
    spread = lax.all_to_all(spread, AXES, split_axis=0, concat_axis=0, tiled=True)

    device = 2 * ctx_index + lax.axis_index("head")
    base = (device // half) * half
    wanted = base + jnp.arange(half, dtype=jnp.int32)
    chips = jnp.arange(spans, dtype=jnp.int32) // 2
    holder = jnp.sum(jnp.where(span_order[None, :] == wanted[:, None], chips[None, :], 0), axis=1)
    spread = spread.reshape(half, 2, 2, piece, width)
    routed = jnp.take(spread, holder, axis=0, mode="clip")
    groups = [list(range(half)), list(range(half, spans))]
    routed = lax.all_to_all(
        routed, AXES, split_axis=0, concat_axis=0, tiled=True, axis_index_groups=groups
    )
    rows = routed.transpose(2, 0, 3, 1, 4).reshape(2, per_span, PAGE, 2 * width)
    slots = lax.dynamic_slice_in_dim(page_table, device * per_span, per_span) - device * per_span
    order = jnp.sum(
        jnp.where(
            slots[None, :] == jnp.arange(per_span, dtype=jnp.int32)[:, None],
            jnp.arange(per_span, dtype=jnp.int32)[None, :],
            0,
        ),
        axis=1,
    )
    return jnp.take(rows, order, axis=1, mode="clip")


def per_device(keys_values, span_order, page_table):
    chips = lax.axis_size("ctx")
    piece = keys_values.shape[1] // chips
    whole_tiles = piece % SUBLANES == 0 and PAGE % piece == 0
    if chips & (chips - 1) == 0 and whole_tiles:
        return by_permutes(keys_values, span_order, page_table)
    return by_all_to_alls(keys_values, span_order, page_table)


def solution(mesh):
    in_specs = (P(None, ("groups", "ctx"), "head"), P("groups"), P("groups"))
    out_specs = P(None, ("groups", "ctx", "head"), None, None)
    return jax.shard_map(
        per_device, mesh=mesh, in_specs=in_specs, out_specs=out_specs, check_vma=False
    )
```

```python
import functools

import jax
import jax.numpy as jnp
from jax import lax
from jax.experimental import pallas as pl
from jax.experimental.pallas import tpu as pltpu
from jax.sharding import PartitionSpec as P

PAGE = 128
SUBLANES = 16
AXES = ("ctx", "head")
VMEM = pl.BlockSpec(memory_space=pltpu.VMEM)
SMEM = pl.BlockSpec(memory_space=pltpu.SMEM)
SMALL = pltpu.CompilerParams(vmem_limit_bytes=8 << 20)
HBM = pl.BlockSpec(memory_space=pltpu.HBM)


def swap(x, distance, size):
    return lax.ppermute(x, AXES, [(i, i ^ distance) for i in range(size)])


def prepare(chips, piece, spans, data, *refs):
    outs, table, table_sem, sems = refs[:-3], *refs[-3:]
    near = chips // 2
    me = lax.axis_index("ctx")
    load = pltpu.make_async_copy(spans, table, table_sem)
    load.start()
    load.wait()
    mine_low = me < near
    first_low = table[2 * me] < chips
    stay = jnp.where(mine_low == first_low, 0, 1)
    rows = near * piece
    copies = []

    def piece_at(block, target):
        start = block * rows + lax.rem(target, near) * piece
        return pl.ds(pl.multiple_of(start, piece), piece)

    n = 0
    for kind in range(2):
        for d in range(near, chips):
            src = data.at[kind, piece_at(1 - stay, me ^ d), :]
            copies.append(pltpu.make_async_copy(src, outs[n], sems.at[n]))
            n += 1
    for d in range(near):
        src = data.at[:, piece_at(stay, me ^ d), :]
        copies.append(pltpu.make_async_copy(src, outs[n], sems.at[n]))
        n += 1
    for copy in copies:
        copy.start()
    for copy in copies:
        copy.wait()


def route(chips, kind, spans, *refs):
    near = chips // 2
    ins, outs = refs[:chips], refs[chips:]
    me = lax.axis_index("ctx")
    local = lax.rem(me, near)
    low = me < near
    for d in range(chips):
        source = me ^ d
        a, b = spans[2 * source], spans[2 * source + 1]
        span = jnp.where((a < chips) == low, a, b)
        parity = lax.rem(span, 2)
        distance = lax.rem(span // 2, near) ^ local
        for j in range(near):

            @pl.when(distance == j)
            def _(d=d, j=j):
                outs[j][parity] = ins[d][kind] if d < near else ins[d][...]


def hand_over(near, *refs):
    ins, out = refs[:near], refs[near]
    other = 1 - lax.axis_index("head")
    for j in range(near):
        out[j] = ins[j][other]


def finish(near, piece, table, *refs):
    per_span = near * piece // PAGE
    own = [refs[:near], refs[near : 2 * near]]
    got = refs[2 * near : 2 * near + 2]
    out, sems = refs[2 * near + 2 :]
    me = lax.axis_index("ctx")
    head = lax.axis_index("head")
    width = out.shape[3] // 2
    device = 2 * me + head
    local = lax.rem(me, near)
    copies = []
    for kind in range(2):
        for j in range(near):
            row = (local ^ j) * piece
            slot = table[device * per_span + row // PAGE] - device * per_span
            rows = pl.ds(pl.multiple_of(lax.rem(row, PAGE), piece), piece)
            for src, side in ((own[kind][j].at[head], head), (got[kind].at[j], 1 - head)):
                cols = pl.ds(pl.multiple_of(side * width, width), width)
                dst = out.at[kind, slot, rows, cols]
                copies.append(pltpu.make_async_copy(src, dst, sems.at[len(copies)]))
    for copy in copies:
        copy.start()
    for copy in copies:
        copy.wait()


def by_permutes(keys_values, span_order, page_table):
    chips = lax.axis_size("ctx")
    size = 2 * chips
    near = chips // 2
    width = keys_values.shape[2]
    span_len = keys_values.shape[1] // 2
    piece = span_len // near
    dtype = keys_values.dtype
    one = jax.ShapeDtypeStruct((piece, width), dtype)
    two = jax.ShapeDtypeStruct((2, piece, width), dtype)
    n = 2 * near + near
    pieces = pl.pallas_call(
        functools.partial(prepare, chips, piece),
        out_shape=[one] * (2 * near) + [two] * near,
        in_specs=[HBM, HBM],
        out_specs=[VMEM] * n,
        scratch_shapes=[
            pltpu.SMEM(span_order.shape, span_order.dtype),
            pltpu.SemaphoreType.DMA,
            pltpu.SemaphoreType.DMA((n,)),
        ],
        name="prepare",
            compiler_params=SMALL,
    )(
        pltpu.with_memory_space_constraint(span_order, pltpu.HBM),
        pltpu.with_memory_space_constraint(keys_values, pltpu.HBM),
    )
    far = [
        [swap(pieces[kind * near + i], 2 * (near + i), size) for i in range(near)]
        for kind in range(2)
    ]
    stay = [pieces[2 * near]] + [
        swap(pieces[2 * near + d], 2 * d, size) for d in range(1, near)
    ]
    own, got = [], []
    for kind in range(2):
        routed = pl.pallas_call(
            functools.partial(route, chips, kind),
            out_shape=[two] * near,
            in_specs=[SMEM] + [VMEM] * chips,
            out_specs=[VMEM] * near,
            name="route",
            compiler_params=SMALL,
        )(span_order, *stay, *far[kind])
        held = [routed[0]] + [swap(routed[j], 2 * j, size) for j in range(1, near)]
        send = pl.pallas_call(
            functools.partial(hand_over, near),
            out_shape=jax.ShapeDtypeStruct((near, piece, width), dtype),
            in_specs=[VMEM] * near,
            out_specs=VMEM,
            name="hand_over",
            compiler_params=SMALL,
        )(*held)
        own += held
        got.append(swap(send, 1, size))
    return pl.pallas_call(
        functools.partial(finish, near, piece),
        out_shape=jax.ShapeDtypeStruct((2, span_len // PAGE, PAGE, 2 * width), dtype),
        in_specs=[SMEM] + [VMEM] * (2 * near + 2),
        out_specs=HBM,
        scratch_shapes=[pltpu.SemaphoreType.DMA((4 * near,))],
        name="finish",
            compiler_params=SMALL,
    )(page_table, *own, *got)


def by_all_to_alls(keys_values, span_order, page_table):
    tok_rows = keys_values.shape[1]
    width = keys_values.shape[2]
    span_len = tok_rows // 2
    per_span = span_len // PAGE
    ctx_index = lax.axis_index("ctx")
    spans = lax.axis_size("ctx") * lax.axis_size("head")
    half = spans // 2
    piece = span_len // half

    first_span = lax.dynamic_index_in_dim(span_order, 2 * ctx_index, keepdims=False)
    flip = first_span >= half
    blocks = keys_values.reshape(2, 2, half, piece, width)
    low = jnp.where(flip, blocks[:, 1], blocks[:, 0])
    high = jnp.where(flip, blocks[:, 0], blocks[:, 1])
    spread = jnp.stack([low, high], axis=0).transpose(0, 2, 1, 3, 4)
    spread = spread.reshape(spans, 2, piece, width)
    spread = lax.all_to_all(spread, AXES, split_axis=0, concat_axis=0, tiled=True)

    device = 2 * ctx_index + lax.axis_index("head")
    base = (device // half) * half
    wanted = base + jnp.arange(half, dtype=jnp.int32)
    chips = jnp.arange(spans, dtype=jnp.int32) // 2
    holder = jnp.sum(jnp.where(span_order[None, :] == wanted[:, None], chips[None, :], 0), axis=1)
    spread = spread.reshape(half, 2, 2, piece, width)
    routed = jnp.take(spread, holder, axis=0, mode="clip")
    groups = [list(range(half)), list(range(half, spans))]
    routed = lax.all_to_all(
        routed, AXES, split_axis=0, concat_axis=0, tiled=True, axis_index_groups=groups
    )
    rows = routed.transpose(2, 0, 3, 1, 4).reshape(2, per_span, PAGE, 2 * width)
    slots = lax.dynamic_slice_in_dim(page_table, device * per_span, per_span) - device * per_span
    order = jnp.sum(
        jnp.where(
            slots[None, :] == jnp.arange(per_span, dtype=jnp.int32)[:, None],
            jnp.arange(per_span, dtype=jnp.int32)[None, :],
            0,
        ),
        axis=1,
    )
    return jnp.take(rows, order, axis=1, mode="clip")


def per_device(keys_values, span_order, page_table):
    chips = lax.axis_size("ctx")
    piece = keys_values.shape[1] // chips
    whole_tiles = piece % SUBLANES == 0 and PAGE % piece == 0
    if chips & (chips - 1) == 0 and whole_tiles:
        return by_permutes(keys_values, span_order, page_table)
    return by_all_to_alls(keys_values, span_order, page_table)


def solution(mesh):
    in_specs = (P(None, ("groups", "ctx"), "head"), P("groups"), P("groups"))
    out_specs = P(None, ("groups", "ctx", "head"), None, None)
    return jax.shard_map(
        per_device, mesh=mesh, in_specs=in_specs, out_specs=out_specs, check_vma=False
    )
```

```python
import functools

import jax
import jax.numpy as jnp
from jax import lax
from jax.experimental import pallas as pl
from jax.experimental.pallas import tpu as pltpu
from jax.sharding import PartitionSpec as P

PAGE = 128
SUBLANES = 16
MIN_BYTES = 1 << 16
AXES = ("ctx", "head")
VMEM = pl.BlockSpec(memory_space=pltpu.VMEM)
SMEM = pl.BlockSpec(memory_space=pltpu.SMEM)
SMALL = pltpu.CompilerParams(vmem_limit_bytes=8 << 20)
HBM = pl.BlockSpec(memory_space=pltpu.HBM)


def swap(x, size, distances):
    pairs = [(i, 2 * (i // 2 ^ distances[i % 2]) + i % 2) for i in range(size)]
    return lax.ppermute(x, AXES, pairs)


def trade(x, size):
    return lax.ppermute(x, AXES, [(i, i ^ 1) for i in range(size)])


def prepare(chips, piece, spans, data, *refs):
    outs, table, table_sem, sems = refs[:-3], *refs[-3:]
    near, lanes = chips // 2, chips // 4
    me = lax.axis_index("ctx")
    load = pltpu.make_async_copy(spans, table, table_sem)
    load.start()
    load.wait()
    first_low = table[2 * me] < chips
    stay = jnp.where((me < near) == first_low, 0, 1)
    copies = []

    def rows(block, i):
        return pl.ds(pl.multiple_of((block * lanes + i) * piece, piece), piece)

    for kind in range(2):
        for i in range(lanes):
            copies.append((data.at[kind, rows(1 - stay, i), :], outs[len(copies)]))
    for i in range(lanes):
        copies.append((data.at[:, rows(stay, i), :], outs[len(copies)]))
    copies = [pltpu.make_async_copy(*c, sems.at[n]) for n, c in enumerate(copies)]
    for copy in copies:
        copy.start()
    for copy in copies:
        copy.wait()


def route(chips, kind, spans, *refs):
    near, lanes = chips // 2, chips // 4
    ins, outs = refs[:chips], refs[chips:]
    me, head = lax.axis_index("ctx"), lax.axis_index("head")
    local, low = lax.rem(me, near), me < near
    for n in range(chips):
        group, i = n // lanes, n % lanes
        core = head if group % 2 == 0 else 1 - head
        source = me ^ ((group // 2) * near + i + core * lanes)
        a, b = spans[2 * source], spans[2 * source + 1]
        span = jnp.where((a < chips) == low, a, b)
        distance = lax.rem(span // 2, near) ^ local
        for j in range(near):

            @pl.when((distance == j) & (lax.rem(span, 2) == head))
            def _(n=n, j=j, group=group):
                outs[j][...] = ins[n][kind] if group < 2 else ins[n][...]


def finish(chips, piece, spans, table, *refs):
    near, lanes = chips // 2, chips // 4
    ins, (out, sems) = refs[: 2 * near], refs[2 * near :]
    pages, width = out.shape[1], out.shape[3] // 2
    me = lax.axis_index("ctx")
    device = 2 * me + lax.axis_index("head")
    source = jnp.int32(0)
    for c in range(chips):
        here = (spans[2 * c] == device) | (spans[2 * c + 1] == device)
        source = jnp.where(here, c, source)
    strip = min(piece, PAGE)
    copies = []
    for n, ref in enumerate(ins):
        kind, j = n // near, n % near
        part = lax.rem(me ^ j ^ source, near)
        cols = pl.ds(pl.multiple_of(part // lanes * width, width), width)
        for k in range(piece // strip):
            row = lax.rem(part, lanes) * piece + k * strip
            slot = table[device * pages + row // PAGE] - device * pages
            rows = pl.ds(pl.multiple_of(lax.rem(row, PAGE), strip), strip)
            src = ref.at[pl.ds(k * strip, strip), :]
            dst = out.at[kind, slot, rows, cols]
            copies.append(pltpu.make_async_copy(src, dst, sems.at[len(copies)]))
    for copy in copies:
        copy.start()
    for copy in copies:
        copy.wait()


def piece_rows(chips, span_len):
    return span_len // max(chips // 4, 1)


def by_permutes(keys_values, span_order, page_table):
    chips = lax.axis_size("ctx")
    size, near, lanes = 2 * chips, chips // 2, chips // 4
    width = keys_values.shape[2]
    span_len = keys_values.shape[1] // 2
    piece = piece_rows(chips, span_len)
    dtype = keys_values.dtype
    one = jax.ShapeDtypeStruct((piece, width), dtype)
    two = jax.ShapeDtypeStruct((2, piece, width), dtype)
    n = 3 * lanes
    pieces = pl.pallas_call(
        functools.partial(prepare, chips, piece),
        out_shape=[one] * (2 * lanes) + [two] * lanes,
        in_specs=[HBM, HBM],
        out_specs=[VMEM] * n,
        scratch_shapes=[
            pltpu.SMEM(span_order.shape, span_order.dtype),
            pltpu.SemaphoreType.DMA,
            pltpu.SemaphoreType.DMA((n,)),
        ],
        name="prepare",
        compiler_params=SMALL,
    )(
        pltpu.with_memory_space_constraint(span_order, pltpu.HBM),
        pltpu.with_memory_space_constraint(keys_values, pltpu.HBM),
    )
    far = [
        [swap(pieces[kind * lanes + i], size, (near + i, near + i + lanes)) for i in range(lanes)]
        for kind in range(2)
    ]
    stay = [swap(pieces[2 * lanes + i], size, (i, i + lanes)) for i in range(lanes)]
    far_other = [[trade(far[kind][i], size) for i in range(lanes)] for kind in range(2)]
    stay_other = [trade(stay[i], size) for i in range(lanes)]
    held = []
    for kind in range(2):
        routed = pl.pallas_call(
            functools.partial(route, chips, kind),
            out_shape=[one] * near,
            in_specs=[SMEM] + [VMEM] * chips,
            out_specs=[VMEM] * near,
            name="route",
            compiler_params=SMALL,
        )(span_order, *stay, *stay_other, *far[kind], *far_other[kind])
        held += [routed[0]] + [swap(routed[j], size, (j, j)) for j in range(1, near)]
    return pl.pallas_call(
        functools.partial(finish, chips, piece),
        out_shape=jax.ShapeDtypeStruct((2, span_len // PAGE, PAGE, 2 * width), dtype),
        in_specs=[SMEM, SMEM] + [VMEM] * (2 * near),
        out_specs=HBM,
        scratch_shapes=[pltpu.SemaphoreType.DMA((2 * near * max(piece // PAGE, 1),))],
        name="finish",
        compiler_params=SMALL,
    )(span_order, page_table, *held)


def by_all_to_alls(keys_values, span_order, page_table):
    tok_rows = keys_values.shape[1]
    width = keys_values.shape[2]
    span_len = tok_rows // 2
    per_span = span_len // PAGE
    ctx_index = lax.axis_index("ctx")
    spans = lax.axis_size("ctx") * lax.axis_size("head")
    half = spans // 2
    piece = span_len // half

    first_span = lax.dynamic_index_in_dim(span_order, 2 * ctx_index, keepdims=False)
    flip = first_span >= half
    blocks = keys_values.reshape(2, 2, half, piece, width)
    low = jnp.where(flip, blocks[:, 1], blocks[:, 0])
    high = jnp.where(flip, blocks[:, 0], blocks[:, 1])
    spread = jnp.stack([low, high], axis=0).transpose(0, 2, 1, 3, 4)
    spread = spread.reshape(spans, 2, piece, width)
    spread = lax.all_to_all(spread, AXES, split_axis=0, concat_axis=0, tiled=True)

    device = 2 * ctx_index + lax.axis_index("head")
    base = (device // half) * half
    wanted = base + jnp.arange(half, dtype=jnp.int32)
    chips = jnp.arange(spans, dtype=jnp.int32) // 2
    holder = jnp.sum(jnp.where(span_order[None, :] == wanted[:, None], chips[None, :], 0), axis=1)
    spread = spread.reshape(half, 2, 2, piece, width)
    routed = jnp.take(spread, holder, axis=0, mode="clip")
    groups = [list(range(half)), list(range(half, spans))]
    routed = lax.all_to_all(
        routed, AXES, split_axis=0, concat_axis=0, tiled=True, axis_index_groups=groups
    )
    rows = routed.transpose(2, 0, 3, 1, 4).reshape(2, per_span, PAGE, 2 * width)
    slots = lax.dynamic_slice_in_dim(page_table, device * per_span, per_span) - device * per_span
    order = jnp.sum(
        jnp.where(
            slots[None, :] == jnp.arange(per_span, dtype=jnp.int32)[:, None],
            jnp.arange(per_span, dtype=jnp.int32)[None, :],
            0,
        ),
        axis=1,
    )
    return jnp.take(rows, order, axis=1, mode="clip")


def pipelined(chips, rows, width, itemsize):
    piece = piece_rows(chips, rows // 2)
    whole = chips >= 4 and chips & (chips - 1) == 0 and piece % SUBLANES == 0
    return whole and piece * width * itemsize >= MIN_BYTES


def per_device(keys_values, span_order, page_table):
    _, rows, width = keys_values.shape
    if pipelined(lax.axis_size("ctx"), rows, width, keys_values.dtype.itemsize):
        return by_permutes(keys_values, span_order, page_table)
    return by_all_to_alls(keys_values, span_order, page_table)


def solution(mesh):
    in_specs = (P(None, ("groups", "ctx"), "head"), P("groups"), P("groups"))
    out_specs = P(None, ("groups", "ctx", "head"), None, None)
    return jax.shard_map(
        per_device, mesh=mesh, in_specs=in_specs, out_specs=out_specs, check_vma=False
    )
```
